32 devices in a mesh: groups: 2 (over y), space: 4 (over z), shot: 4 (over x, core).
Axes of the slice: x: 2, y: 2, z: 4, core: 2. Of those that a mesh axis runs over, the one named last changes fastest.
Arguments:
- wavefields: float32 [8, 2, 2, 64, 16, 256], P(('groups', 'shot'), None, None, 'space'), parts along dimension 0, may hold values from -6 to 6
- velocity: float32 [128, 16, 256], P(('groups', 'space'), 'shot'), parts along dimension 0, may hold values from 0.05 to 0.18
- aperture: int32 [8, 2], P(('groups', 'shot')), parts along dimension 0, may hold values from 0 to 64, as said below
Outputs:
- final_fields: float32 [8, 2, 2, 64, 16, 256], P(('groups', 'shot'), None, None, 'space'), parts along dimension 0
- image: float32 [128, 16, 256], P(('groups', 'space'), 'shot'), parts along dimension 0
The draws below stay inside these ranges and needn't reach their ends.
There are 2 independent parts, one for each index of `groups`. The reference program is written for one: setup_inputs(seed, part) draws one part's arguments, and reference() takes and returns one part's arrays. A program takes and returns all parts, laid end to end along the dimension named above; each array names one. Nothing has to cross between parts.
Inputs may be any that keep to these rules, and one draw needn't show every extreme that they name: Row s holds shot s's aperture [lo, hi): lo below 16 and hi above 48.
All inputs are finite; a program needn't handle non-finite values.
Results may differ from the reference program's by a relative error of at most 0.0003.
Values sent between devices are 32-bit elements; how exact they have to be, the bound alone decides.
A program may use at most 64 MiB of HBM per device.

```python
import jax
import jax.numpy as jnp
from jax import lax

Y = 16
Z = 256
STEPS = 8
SHOTS = 4
X = 64


def draw_aperture(key, part):
    first_key, second_key = jax.random.split(jax.random.fold_in(key, 7))
    lower = jax.random.randint(first_key, (SHOTS,), 0, X // 4)
    upper = X - jax.random.randint(second_key, (SHOTS,), 0, X // 4)
    return jnp.stack([lower, upper], axis=1).astype(jnp.int32)


def level_of(stream_key, dims, cuts, smallest, high):
    factor_of = 1.0
    for axis_at, shards_of in cuts:
        steps = jax.random.uniform(jax.random.fold_in(jax.random.fold_in(stream_key, 6), axis_at), (shards_of,), jnp.float32, smallest / len(cuts), high / len(cuts))
        factor_of = factor_of * jnp.repeat(jnp.exp(steps), dims[axis_at] // shards_of).reshape((-1,) + (1,) * (len(dims) - 1 - axis_at))
    return factor_of


def scatter_about(own_key, dims, spread, most, cuts=(), held_as=jnp.bfloat16):
    drawn = jax.random.normal(own_key, dims, jnp.float32) * spread
    if len(cuts) > 0:
        drawn = level_of(own_key, dims, cuts, -0.22, 0.18) * drawn
    return jnp.clip(drawn, min=-most, max=most).astype(held_as)


def setup_inputs(seed: int = 0, part: int = 0) -> dict:
    key_list = jax.random.split(jax.random.key(seed), 4)
    part_splits = jax.random.split(jax.random.fold_in(key_list[3], part), 4)
    wavefields = scatter_about(part_splits[0], (SHOTS, 2, 2, X, Y, Z), 1.0, 6.0, ((0, 4), (3, 4)), jnp.float32)
    velocity = jnp.clip(0.05 + 0.13000001 * jax.random.uniform(part_splits[1], (X, Y, Z), jnp.float32) ** level_of(part_splits[1], (X, Y, Z), ((0, 4), (1, 4)), -0.2, 0.2), 0.05, 0.18)
    aperture = draw_aperture(jax.random.fold_in(jax.random.fold_in(key_list[3], part), 71), part)
    return {"wavefields": wavefields, "velocity": velocity, "aperture": aperture}


coefficients = (-205.0 / 72.0, 8.0 / 5.0, -1.0 / 5.0, 8.0 / 315.0, -1.0 / 560.0)


def laplace(padded):
    rows_x = padded.shape[1] - 8
    rows_y = padded.shape[2]
    rows_z = padded.shape[3]
    padded_all = jnp.pad(padded, ((0, 0), (0, 0), (4, 4), (4, 4)))
    center = padded_all[:, 4:4 + rows_x, 4:4 + rows_y, 4:4 + rows_z]
    summed = (3.0 * coefficients[0]) * center
    for reach in range(1, 5):
        beside_all = padded_all[:, 4 + reach:4 + reach + rows_x, 4:4 + rows_y, 4:4 + rows_z]
        beside_all = beside_all + padded_all[:, 4 - reach:4 - reach + rows_x, 4:4 + rows_y, 4:4 + rows_z]
        beside_all = beside_all + padded_all[:, 4:4 + rows_x, 4 + reach:4 + reach + rows_y, 4:4 + rows_z]
        beside_all = beside_all + padded_all[:, 4:4 + rows_x, 4 - reach:4 - reach + rows_y, 4:4 + rows_z]
        beside_all = beside_all + padded_all[:, 4:4 + rows_x, 4:4 + rows_y, 4 + reach:4 + reach + rows_z]
        beside_all = beside_all + padded_all[:, 4:4 + rows_x, 4:4 + rows_y, 4 - reach:4 - reach + rows_z]
        summed = summed + coefficients[reach] * beside_all
    return summed


def reference(wavefields, velocity, aperture):
    def one_shot(packed):
        fields, bounds = packed
        previous = fields[0]
        current = fields[1]
        global_x = jnp.arange(X, dtype=jnp.int32)
        inside = ((global_x >= bounds[0]) & (global_x < bounds[1])).astype(jnp.float32)[:, None, None]
        partial_value = jnp.zeros((X, Y, Z), jnp.float32)
        for step_index in range(STEPS):
            padded = jnp.pad(current, ((0, 0), (4, 4), (0, 0), (0, 0)))
            following = inside * (2.0 * current - previous + velocity * laplace(padded))
            partial_value = partial_value + following[0] * following[1]
            previous = current
            current = following
        return jnp.stack([previous, current]), partial_value

    finals, partials = lax.map(one_shot, (wavefields, aperture))
    return finals, jnp.sum(partials, axis=0) / STEPS
```

```python
import functools

import jax
import jax.numpy as jnp
import numpy as np
from jax import lax
from jax.experimental import pallas as pl
from jax.experimental.pallas import tpu as pltpu
from jax.sharding import PartitionSpec as P

STEPS = 8
REACH = 4


coefficients = (-205.0 / 72.0, 8.0 / 5.0, -1.0 / 5.0, 8.0 / 315.0, -1.0 / 560.0)


def band(size):
    matrix = np.zeros((size, size), np.float32)
    for reach in range(1, REACH + 1):
        matrix += np.float32(coefficients[reach]) * (
            np.eye(size, k=reach, dtype=np.float32) + np.eye(size, k=-reach, dtype=np.float32)
        )
    return matrix


def split(matrix, axis):
    high = matrix.astype(jnp.bfloat16)
    low = (matrix - high.astype(np.float32)).astype(jnp.bfloat16)
    return np.concatenate([high, high, low], axis=axis)


def kernel(
    left_ref, right_ref, waves, velocity, aperture, out, image,
    halo, speeds, speed, inside, lap, total, parts, arrived,
    halo_send, halo_recv, speed_send, speed_recv, part_send, part_recv, local_sem,
):
    space = lax.axis_index("space")
    spaces = lax.axis_size("space")
    shot = lax.axis_index("shot")
    shots = lax.axis_size("shot")
    cells_x, rows_y, rows_z = out.shape[2:]
    slab = velocity.shape[1]
    flat = (cells_x * rows_y, rows_z)
    has_left = space > 0
    has_right = space < spaces - 1

    load = pltpu.make_async_copy(waves, out, local_sem.at[0])
    load.start()
    own_speed = pltpu.make_async_copy(velocity, speeds.at[shot], local_sem.at[1])
    own_speed.start()

    barrier = pltpu.get_barrier_semaphore()

    @pl.when(has_left)
    def _():
        pl.semaphore_signal(barrier, inc=1, device_id={"space": space - 1}, device_id_type=pl.DeviceIdType.MESH)

    @pl.when(has_right)
    def _():
        pl.semaphore_signal(barrier, inc=1, device_id={"space": space + 1}, device_id_type=pl.DeviceIdType.MESH)

    for ahead in range(1, shots):
        peer = lax.rem(shot + ahead, shots)
        pl.semaphore_signal(barrier, inc=1, device_id={"shot": peer}, device_id_type=pl.DeviceIdType.MESH)
    pl.semaphore_wait(barrier, shots - 1 + jnp.where(has_left, 1, 0) + jnp.where(has_right, 1, 0))

    def to_right(source, slot, field):
        return pltpu.make_async_remote_copy(
            source.at[field, cells_x - REACH : cells_x],
            halo.at[slot, field, 0],
            halo_send.at[slot, field, 0],
            halo_recv.at[slot, field, 0],
            device_id={"space": space + 1},
            device_id_type=pl.DeviceIdType.MESH,
        )

    def to_left(source, slot, field):
        return pltpu.make_async_remote_copy(
            source.at[field, 0:REACH],
            halo.at[slot, field, 1],
            halo_send.at[slot, field, 1],
            halo_recv.at[slot, field, 1],
            device_id={"space": space - 1},
            device_id_type=pl.DeviceIdType.MESH,
        )

    def send(source, slot, field):
        @pl.when(has_right)
        def _():
            to_right(source, slot, field).start()

        @pl.when(has_left)
        def _():
            to_left(source, slot, field).start()

    def sent(source, slot, field):
        @pl.when(has_right)
        def _():
            to_right(source, slot, field).wait_send()

        @pl.when(has_left)
        def _():
            to_left(source, slot, field).wait_send()

    def received(source, slot, field):
        @pl.when(has_left)
        def _():
            to_right(source, slot, field).wait_recv()

        @pl.when(has_right)
        def _():
            to_left(source, slot, field).wait_recv()

    send(waves.at[1], 0, 0)
    send(waves.at[1], 0, 1)

    speed_copies = []
    for ahead in range(1, shots):
        peer = lax.rem(shot + ahead, shots)
        copy = pltpu.make_async_remote_copy(
            velocity,
            speeds.at[shot],
            speed_send.at[ahead - 1],
            speed_recv.at[ahead - 1],
            device_id={"shot": peer},
            device_id_type=pl.DeviceIdType.MESH,
        )
        copy.start()
        speed_copies.append(copy)

    @pl.when(jnp.logical_not(has_left))
    def _():
        halo[:, :, 0] = jnp.zeros((STEPS, 2, REACH, rows_y, rows_z), jnp.float32)

    @pl.when(jnp.logical_not(has_right))
    def _():
        halo[:, :, 1] = jnp.zeros((STEPS, 2, REACH, rows_y, rows_z), jnp.float32)

    total[...] = jnp.zeros(total.shape, jnp.float32)
    global_x = space * cells_x + lax.broadcasted_iota(jnp.int32, inside.shape, 0)
    within = (global_x >= aperture[0, 0]) & (global_x < aperture[0, 1])
    inside[...] = jnp.where(within, 1.0, 0.0)

    load.wait()
    own_speed.wait()
    for copy in speed_copies:
        copy.wait()
    for index in range(shots):
        rows = slice(index * slab, (index + 1) * slab)
        speed[:, rows, :] = speeds[index]
    speed[...] = speed[...] * inside[...]

    def spread(now, field):
        cells = out[now, field].reshape(flat)
        high = cells.astype(jnp.bfloat16)
        low = (cells - high.astype(jnp.float32)).astype(jnp.bfloat16)
        lap[...] = (
            jnp.dot(left_ref[...], jnp.concatenate([high, low, high], axis=0), preferred_element_type=jnp.float32)
            + jnp.dot(jnp.concatenate([high, low, high], axis=1), right_ref[...], preferred_element_type=jnp.float32)
            + (3.0 * coefficients[0]) * cells
        ).reshape(lap.shape)

    def advance(now, then, field, start, stop, beside=None):
        cells = slice(start, stop)
        summed = lap[cells]
        if beside is not None:
            summed = summed + beside
        following = (
            inside[cells] * (2.0 * out[now, field, cells] - out[then, field, cells])
            + speed[cells] * summed
        )
        out[then, field, cells] = following
        if field == 1:
            total[cells] = total[cells] + out[then, 0, cells] * following

    def step(index, carry):
        then = lax.rem(index, 2)
        now = 1 - then
        for field in range(2):
            spread(now, field)

            @pl.when(index > 1)
            def _():
                sent(out.at[then], index - 1, field)

            @pl.when(index == 1)
            def _():
                sent(waves.at[1], 0, field)

            advance(now, then, field, REACH, cells_x - REACH)
            received(out.at[now], index, field)
            for cell in range(REACH):
                beside = sum(
                    coefficients[cell + REACH - layer] * halo[index, field, 0, layer]
                    for layer in range(cell, REACH)
                )
                advance(now, then, field, cell, cell + 1, beside[None])
                beside = sum(
                    coefficients[REACH + layer - cell] * halo[index, field, 1, layer]
                    for layer in range(cell + 1)
                )
                at = cells_x - REACH + cell
                advance(now, then, field, at, at + 1, beside[None])

            @pl.when(index < STEPS - 1)
            def _():
                send(out.at[then], index + 1, field)

        return carry

    lax.fori_loop(0, STEPS, step, 0)

    for index in range(shots):
        rows = slice(index * slab, (index + 1) * slab)
        parts[index] = total[:, rows, :]
    part_copies = []
    for ahead in range(1, shots):
        peer = lax.rem(shot + ahead, shots)
        copy = pltpu.make_async_remote_copy(
            parts.at[peer],
            arrived.at[ahead - 1],
            part_send.at[ahead - 1],
            part_recv.at[ahead - 1],
            device_id={"shot": peer},
            device_id_type=pl.DeviceIdType.MESH,
        )
        copy.start()
        part_copies.append(copy)
    for field in range(2):
        sent(out.at[(STEPS - 2) % 2], STEPS - 1, field)
    summed = parts[shot]
    for ahead in range(1, shots):
        part_copies[ahead - 1].wait()
        summed = summed + arrived[ahead - 1]
    image[...] = summed / STEPS


def shards(wavefields, velocity, aperture):
    fields = wavefields[0]
    cells_x, rows_y, rows_z = fields.shape[2:]
    shots = lax.axis_size("shot")
    slab = velocity.shape[1]
    left = split(
        np.kron(band(cells_x), np.eye(rows_y, dtype=np.float32))
        + np.kron(np.eye(cells_x, dtype=np.float32), band(rows_y)),
        1,
    )
    right = split(band(rows_z), 0)
    grid = (cells_x, rows_y, rows_z)
    vmem = pl.BlockSpec(memory_space=pltpu.VMEM)
    anywhere = pl.BlockSpec(memory_space=pl.ANY)
    finals, image = pl.pallas_call(
        kernel,
        out_shape=(
            jax.ShapeDtypeStruct(fields.shape, jnp.float32),
            jax.ShapeDtypeStruct(velocity.shape, jnp.float32),
        ),
        in_specs=[vmem, vmem, anywhere, anywhere, pl.BlockSpec(memory_space=pltpu.SMEM)],
        out_specs=(vmem, vmem),
        scratch_shapes=[
            pltpu.VMEM((STEPS, 2, 2, REACH, rows_y, rows_z), jnp.float32),
            pltpu.VMEM((shots,) + velocity.shape, jnp.float32),
            pltpu.VMEM(grid, jnp.float32),
            pltpu.VMEM(grid, jnp.float32),
            pltpu.VMEM(grid, jnp.float32),
            pltpu.VMEM(grid, jnp.float32),
            pltpu.VMEM((shots,) + velocity.shape, jnp.float32),
            pltpu.VMEM((shots - 1,) + velocity.shape, jnp.float32),
            pltpu.SemaphoreType.DMA((STEPS, 2, 2)),
            pltpu.SemaphoreType.DMA((STEPS, 2, 2)),
            pltpu.SemaphoreType.DMA((shots - 1,)),
            pltpu.SemaphoreType.DMA((shots - 1,)),
            pltpu.SemaphoreType.DMA((shots - 1,)),
            pltpu.SemaphoreType.DMA((shots - 1,)),
            pltpu.SemaphoreType.DMA((2,)),
        ],
        compiler_params=pltpu.CompilerParams(collective_id=0, has_side_effects=True),
    )(jnp.asarray(left), jnp.asarray(right), fields, velocity, aperture)
    return finals[None], image


def solution(mesh):
    in_specs = (
        P(("groups", "shot"), None, None, "space", None, None),
        P(("groups", "space"), "shot", None),
        P(("groups", "shot"), None),
    )
    out_specs = (
        P(("groups", "shot"), None, None, "space", None, None),
        P(("groups", "space"), "shot", None),
    )
    return jax.shard_map(shards, mesh=mesh, in_specs=in_specs, out_specs=out_specs, check_vma=False)
```

```python
import functools

import jax
import jax.numpy as jnp
import numpy as np
from jax import lax
from jax.experimental import pallas as pl
from jax.experimental.pallas import tpu as pltpu
from jax.sharding import PartitionSpec as P

STEPS = 8
REACH = 4


coefficients = (-205.0 / 72.0, 8.0 / 5.0, -1.0 / 5.0, 8.0 / 315.0, -1.0 / 560.0)


def band(size):
    matrix = np.zeros((size, size), np.float32)
    for reach in range(1, REACH + 1):
        matrix += np.float32(coefficients[reach]) * (
            np.eye(size, k=reach, dtype=np.float32) + np.eye(size, k=-reach, dtype=np.float32)
        )
    return matrix


def split(matrix, axis):
    high = matrix.astype(jnp.bfloat16)
    low = (matrix - high.astype(np.float32)).astype(jnp.bfloat16)
    return np.concatenate([high, high, low], axis=axis)


def kernel(
    left, right, waves, velocity, aperture, finals, image,
    left_ref, right_ref, out, halo, speeds, speed, inside, lap, total,
    middle, middle_arrived, edges, edges_arrived,
    halo_send, halo_recv, speed_send, speed_recv, part_send, part_recv, local_sem,
):
    space = lax.axis_index("space")
    spaces = lax.axis_size("space")
    shot = lax.axis_index("shot")
    shots = lax.axis_size("shot")
    cells_x, rows_y, rows_z = out.shape[2:]
    slab = velocity.shape[1]
    flat = (cells_x * rows_y, rows_z)
    has_left = space > 0
    has_right = space < spaces - 1

    load = pltpu.make_async_copy(waves, out, local_sem.at[0])
    load.start()
    load_left = pltpu.make_async_copy(left, left_ref, local_sem.at[2])
    load_left.start()
    load_right = pltpu.make_async_copy(right, right_ref, local_sem.at[3])
    load_right.start()
    own_speed = pltpu.make_async_copy(velocity, speeds.at[shot], local_sem.at[1])
    own_speed.start()

    barrier = pltpu.get_barrier_semaphore()

    @pl.when(has_left)
    def _():
        pl.semaphore_signal(barrier, inc=1, device_id={"space": space - 1}, device_id_type=pl.DeviceIdType.MESH)

    @pl.when(has_right)
    def _():
        pl.semaphore_signal(barrier, inc=1, device_id={"space": space + 1}, device_id_type=pl.DeviceIdType.MESH)

    for ahead in range(1, shots):
        peer = lax.rem(shot + ahead, shots)
        pl.semaphore_signal(barrier, inc=1, device_id={"shot": peer}, device_id_type=pl.DeviceIdType.MESH)
    pl.semaphore_wait(barrier, shots - 1 + jnp.where(has_left, 1, 0) + jnp.where(has_right, 1, 0))

    def to_right(source, slot, field):
        return pltpu.make_async_remote_copy(
            source.at[field, cells_x - REACH : cells_x],
            halo.at[slot, field, 0],
            halo_send.at[slot, field, 0],
            halo_recv.at[slot, field, 0],
            device_id={"space": space + 1},
            device_id_type=pl.DeviceIdType.MESH,
        )

    def to_left(source, slot, field):
        return pltpu.make_async_remote_copy(
            source.at[field, 0:REACH],
            halo.at[slot, field, 1],
            halo_send.at[slot, field, 1],
            halo_recv.at[slot, field, 1],
            device_id={"space": space - 1},
            device_id_type=pl.DeviceIdType.MESH,
        )

    def send(source, slot, field, side):
        if side == 0:
            @pl.when(has_left)
            def _():
                to_left(source, slot, field).start()
        else:
            @pl.when(has_right)
            def _():
                to_right(source, slot, field).start()

    def sent(source, slot, field):
        @pl.when(has_right)
        def _():
            to_right(source, slot, field).wait_send()

        @pl.when(has_left)
        def _():
            to_left(source, slot, field).wait_send()

    def received(source, slot, field, side):
        if side == 0:
            @pl.when(has_left)
            def _():
                to_right(source, slot, field).wait_recv()
        else:
            @pl.when(has_right)
            def _():
                to_left(source, slot, field).wait_recv()

    for field in range(2):
        for side in range(2):
            send(waves.at[1], 0, field, side)

    speed_copies = []
    for ahead in range(1, shots):
        peer = lax.rem(shot + ahead, shots)
        copy = pltpu.make_async_remote_copy(
            velocity,
            speeds.at[shot],
            speed_send.at[ahead - 1],
            speed_recv.at[ahead - 1],
            device_id={"shot": peer},
            device_id_type=pl.DeviceIdType.MESH,
        )
        copy.start()
        speed_copies.append(copy)

    @pl.when(jnp.logical_not(has_left))
    def _():
        halo[:, :, 0] = jnp.zeros((STEPS, 2, REACH, rows_y, rows_z), jnp.float32)

    @pl.when(jnp.logical_not(has_right))
    def _():
        halo[:, :, 1] = jnp.zeros((STEPS, 2, REACH, rows_y, rows_z), jnp.float32)

    total[...] = jnp.zeros(total.shape, jnp.float32)
    global_x = space * cells_x + lax.broadcasted_iota(jnp.int32, inside.shape, 0)
    within = (global_x >= aperture[0, 0]) & (global_x < aperture[0, 1])
    inside[...] = jnp.where(within, 1.0, 0.0)

    def spread(now, field):
        cells = out[now, field].reshape(flat)
        high = cells.astype(jnp.bfloat16)
        low = (cells - high.astype(jnp.float32)).astype(jnp.bfloat16)
        lap[field] = (
            jnp.dot(left_ref[...], jnp.concatenate([high, low, high], axis=0), preferred_element_type=jnp.float32)
            + jnp.dot(jnp.concatenate([high, low, high], axis=1), right_ref[...], preferred_element_type=jnp.float32)
            + (3.0 * coefficients[0]) * cells
        ).reshape(lap.shape[1:])

    def advance(now, then, field, start, stop, beside=None):
        cells = slice(start, stop)
        summed = lap[field, cells]
        if beside is not None:
            summed = summed + beside
        following = (
            inside[cells] * (2.0 * out[now, field, cells] - out[then, field, cells])
            + speed[cells] * summed
        )
        out[then, field, cells] = following
        if field == 1:
            total[cells] = total[cells] + out[then, 0, cells] * following

    def border(index, now, then, field, side):
        received(out.at[now], index, field, side)
        for cell in range(REACH):
            if side == 0:
                at = cell
                beside = sum(
                    coefficients[cell + REACH - layer] * halo[index, field, 0, layer]
                    for layer in range(cell, REACH)
                )
            else:
                at = cells_x - REACH + cell
                beside = sum(
                    coefficients[REACH + layer - cell] * halo[index, field, 1, layer]
                    for layer in range(cell + 1)
                )
            advance(now, then, field, at, at + 1, beside[None])

    def step(index, carry):
        then = lax.rem(index, 2)
        now = 1 - then
        for field in range(2):
            @pl.when(index > 1)
            def _():
                sent(out.at[then], index - 1, field)

            @pl.when(index == 1)
            def _():
                sent(waves.at[1], 0, field)

            advance(now, then, field, REACH, cells_x - REACH)
            for side in range(2):
                border(index, now, then, field, side)
                send(out.at[then], index + 1, field, side)
            spread(then, field)
        return carry

    load.wait()
    load_left.wait()
    load_right.wait()
    spread(1, 0)
    spread(1, 1)
    own_speed.wait()
    for copy in speed_copies:
        copy.wait()
    for index in range(shots):
        rows = slice(index * slab, (index + 1) * slab)
        speed[:, rows, :] = speeds[index]
    speed[...] = speed[...] * inside[...]

    lax.fori_loop(0, STEPS - 1, step, 0)

    last = STEPS - 1
    then = last % 2
    now = 1 - then
    keep_now = pltpu.make_async_copy(out.at[now], finals.at[0], local_sem.at[0])
    keep_now.start()

    def part_copy(kind, source, target, ahead):
        peer = lax.rem(shot + ahead, shots)
        return pltpu.make_async_remote_copy(
            source.at[peer],
            target.at[ahead - 1],
            part_send.at[kind, ahead - 1],
            part_recv.at[kind, ahead - 1],
            device_id={"shot": peer},
            device_id_type=pl.DeviceIdType.MESH,
        )

    for field in range(2):
        sent(out.at[then], last - 1, field)
        advance(now, then, field, REACH, cells_x - REACH)
    for index in range(shots):
        rows = slice(index * slab, (index + 1) * slab)
        middle[index] = total[REACH : cells_x - REACH, rows, :]
    copies = [part_copy(0, middle, middle_arrived, ahead) for ahead in range(1, shots)]
    for copy in copies:
        copy.start()
    for field in range(2):
        for side in range(2):
            border(last, now, then, field, side)
    for index in range(shots):
        rows = slice(index * slab, (index + 1) * slab)
        edges[index, 0:REACH] = total[0:REACH, rows, :]
        edges[index, REACH:] = total[cells_x - REACH :, rows, :]
    edge_copies = [part_copy(1, edges, edges_arrived, ahead) for ahead in range(1, shots)]
    for copy in edge_copies:
        copy.start()
    keep_then = pltpu.make_async_copy(out.at[then], finals.at[1], local_sem.at[1])
    keep_then.start()
    for field in range(2):
        sent(out.at[now], last, field)
    summed = middle[shot]
    for copy, ahead in zip(copies, range(1, shots)):
        copy.wait()
        summed = summed + middle_arrived[ahead - 1]
    image[REACH : cells_x - REACH] = summed / STEPS
    summed = edges[shot]
    for copy, ahead in zip(edge_copies, range(1, shots)):
        copy.wait()
        summed = summed + edges_arrived[ahead - 1]
    image[0:REACH] = summed[0:REACH] / STEPS
    image[cells_x - REACH :] = summed[REACH:] / STEPS
    keep_now.wait()
    keep_then.wait()


def keep(fields, image, fields_out, image_out, fields_held, image_held, load_sem, store_sem):
    pieces = [(image, image_held, image_out)]
    for time in range(2):
        for field in range(2):
            pieces.append(
                (fields.at[time, field], fields_held.at[time, field], fields_out.at[time, field])
            )
    loads = [
        pltpu.make_async_copy(source, held, load_sem.at[at])
        for at, (source, held, _) in enumerate(pieces)
    ]
    stores = [
        pltpu.make_async_copy(held, target, store_sem.at[at])
        for at, (_, held, target) in enumerate(pieces)
    ]
    for load in loads:
        load.start()
    for load, store in zip(loads, stores):
        load.wait()
        store.start()
    for store in stores:
        store.wait()


def shards(wavefields, velocity, aperture):
    fields = wavefields[0]
    cells_x, rows_y, rows_z = fields.shape[2:]
    shots = lax.axis_size("shot")
    slab = velocity.shape[1]
    left = split(
        np.kron(band(cells_x), np.eye(rows_y, dtype=np.float32))
        + np.kron(np.eye(cells_x, dtype=np.float32), band(rows_y)),
        1,
    )
    right = split(band(rows_z), 0)
    grid = (cells_x, rows_y, rows_z)
    vmem = pl.BlockSpec(memory_space=pltpu.VMEM)
    anywhere = pl.BlockSpec(memory_space=pl.ANY)
    finals, image = pl.pallas_call(
        kernel,
        out_shape=(
            jax.ShapeDtypeStruct(fields.shape, jnp.float32),
            jax.ShapeDtypeStruct(velocity.shape, jnp.float32),
        ),
        in_specs=[anywhere, anywhere, anywhere, anywhere, pl.BlockSpec(memory_space=pltpu.SMEM)],
        out_specs=(anywhere, vmem),
        scratch_shapes=[
            pltpu.VMEM(left.shape, jnp.bfloat16),
            pltpu.VMEM(right.shape, jnp.bfloat16),
            pltpu.VMEM(fields.shape, jnp.float32),
            pltpu.VMEM((STEPS, 2, 2, REACH, rows_y, rows_z), jnp.float32),
            pltpu.VMEM((shots,) + velocity.shape, jnp.float32),
            pltpu.VMEM(grid, jnp.float32),
            pltpu.VMEM(grid, jnp.float32),
            pltpu.VMEM((2,) + grid, jnp.float32),
            pltpu.VMEM(grid, jnp.float32),
            pltpu.VMEM((shots, cells_x - 2 * REACH, slab, rows_z), jnp.float32),
            pltpu.VMEM((shots - 1, cells_x - 2 * REACH, slab, rows_z), jnp.float32),
            pltpu.VMEM((shots, 2 * REACH, slab, rows_z), jnp.float32),
            pltpu.VMEM((shots - 1, 2 * REACH, slab, rows_z), jnp.float32),
            pltpu.SemaphoreType.DMA((STEPS, 2, 2)),
            pltpu.SemaphoreType.DMA((STEPS, 2, 2)),
            pltpu.SemaphoreType.DMA((shots - 1,)),
            pltpu.SemaphoreType.DMA((shots - 1,)),
            pltpu.SemaphoreType.DMA((2, shots - 1)),
            pltpu.SemaphoreType.DMA((2, shots - 1)),
            pltpu.SemaphoreType.DMA((4,)),
        ],
        compiler_params=pltpu.CompilerParams(collective_id=0, has_side_effects=True),
    )(jnp.asarray(left), jnp.asarray(right), fields, velocity, aperture)
    finals, image = pl.pallas_call(
        keep,
        out_shape=(
            jax.ShapeDtypeStruct(fields.shape, jnp.float32),
            jax.ShapeDtypeStruct(velocity.shape, jnp.float32),
        ),
        in_specs=[anywhere, anywhere],
        out_specs=(anywhere, anywhere),
        scratch_shapes=[
            pltpu.VMEM(fields.shape, jnp.float32),
            pltpu.VMEM(velocity.shape, jnp.float32),
            pltpu.SemaphoreType.DMA((5,)),
            pltpu.SemaphoreType.DMA((5,)),
        ],
    )(finals, image)
    return finals[None], image


def solution(mesh):
    in_specs = (
        P(("groups", "shot"), None, None, "space", None, None),
        P(("groups", "space"), "shot", None),
        P(("groups", "shot"), None),
    )
    out_specs = (
        P(("groups", "shot"), None, None, "space", None, None),
        P(("groups", "space"), "shot", None),
    )
    return jax.shard_map(shards, mesh=mesh, in_specs=in_specs, out_specs=out_specs, check_vma=False)
```

```python
import functools

import jax
import jax.numpy as jnp
import numpy as np
from jax import lax
from jax.experimental import pallas as pl
from jax.experimental.pallas import tpu as pltpu
from jax.sharding import PartitionSpec as P

STEPS = 8
REACH = 4


coefficients = (-205.0 / 72.0, 8.0 / 5.0, -1.0 / 5.0, 8.0 / 315.0, -1.0 / 560.0)


def band(size):
    matrix = np.zeros((size, size), np.float32)
    for reach in range(1, REACH + 1):
        matrix += np.float32(coefficients[reach]) * (
            np.eye(size, k=reach, dtype=np.float32) + np.eye(size, k=-reach, dtype=np.float32)
        )
    return matrix


def split(matrix, axis):
    high = matrix.astype(jnp.bfloat16)
    low = (matrix - high.astype(np.float32)).astype(jnp.bfloat16)
    return np.concatenate([high, high, low], axis=axis)


def kernel(
    left, right, waves, velocity, aperture, finals, image,
    left_ref, right_ref, out, halo, speeds, speed, inside, lap, total,
    middle, middle_arrived, edges, edges_arrived,
    halo_send, halo_recv, speed_send, speed_recv, part_send, part_recv, local_sem,
):
    space = lax.axis_index("space")
    spaces = lax.axis_size("space")
    shot = lax.axis_index("shot")
    shots = lax.axis_size("shot")
    cells_x, rows_y, rows_z = out.shape[2:]
    slab = velocity.shape[1]
    flat = (cells_x * rows_y, rows_z)
    has_left = space > 0
    has_right = space < spaces - 1

    load = pltpu.make_async_copy(waves, out, local_sem.at[0])
    load.start()
    load_left = pltpu.make_async_copy(left, left_ref, local_sem.at[2])
    load_left.start()
    load_right = pltpu.make_async_copy(right, right_ref, local_sem.at[3])
    load_right.start()
    own_speed = pltpu.make_async_copy(velocity, speeds.at[shot], local_sem.at[1])
    own_speed.start()

    barrier = pltpu.get_barrier_semaphore()

    @pl.when(has_left)
    def _():
        pl.semaphore_signal(barrier, inc=1, device_id={"space": space - 1}, device_id_type=pl.DeviceIdType.MESH)

    @pl.when(has_right)
    def _():
        pl.semaphore_signal(barrier, inc=1, device_id={"space": space + 1}, device_id_type=pl.DeviceIdType.MESH)

    for ahead in range(1, shots):
        peer = lax.rem(shot + ahead, shots)
        pl.semaphore_signal(barrier, inc=1, device_id={"shot": peer}, device_id_type=pl.DeviceIdType.MESH)
    pl.semaphore_wait(barrier, shots - 1 + jnp.where(has_left, 1, 0) + jnp.where(has_right, 1, 0))

    def to_right(source, slot, field):
        return pltpu.make_async_remote_copy(
            source.at[field, cells_x - REACH : cells_x],
            halo.at[slot, field, 0],
            halo_send.at[slot, field, 0],
            halo_recv.at[slot, field, 0],
            device_id={"space": space + 1},
            device_id_type=pl.DeviceIdType.MESH,
        )

    def to_left(source, slot, field):
        return pltpu.make_async_remote_copy(
            source.at[field, 0:REACH],
            halo.at[slot, field, 1],
            halo_send.at[slot, field, 1],
            halo_recv.at[slot, field, 1],
            device_id={"space": space - 1},
            device_id_type=pl.DeviceIdType.MESH,
        )

    def send(source, slot, field, side):
        if side == 0:
            @pl.when(has_left)
            def _():
                to_left(source, slot, field).start()
        else:
            @pl.when(has_right)
            def _():
                to_right(source, slot, field).start()

    def sent(source, slot, field):
        @pl.when(has_right)
        def _():
            to_right(source, slot, field).wait_send()

        @pl.when(has_left)
        def _():
            to_left(source, slot, field).wait_send()

    def received(source, slot, field, side):
        if side == 0:
            @pl.when(has_left)
            def _():
                to_right(source, slot, field).wait_recv()
        else:
            @pl.when(has_right)
            def _():
                to_left(source, slot, field).wait_recv()

    for field in range(2):
        for side in range(2):
            send(waves.at[1], 0, field, side)

    spans = ((0, REACH), (cells_x - REACH, cells_x), (REACH, cells_x - REACH))
    speed_copies = []
    for kind, (start, stop) in enumerate(spans):
        for ahead in range(1, shots):
            peer = lax.rem(shot + ahead, shots)
            copy = pltpu.make_async_remote_copy(
                velocity.at[start:stop],
                speeds.at[shot, start:stop],
                speed_send.at[kind, ahead - 1],
                speed_recv.at[kind, ahead - 1],
                device_id={"shot": peer},
                device_id_type=pl.DeviceIdType.MESH,
            )
            copy.start()
            speed_copies.append(copy)

    def gather(kinds):
        for kind in kinds:
            start, stop = spans[kind]
            for copy in speed_copies[kind * (shots - 1) : (kind + 1) * (shots - 1)]:
                copy.wait()
            for index in range(shots):
                rows = slice(index * slab, (index + 1) * slab)
                speed[start:stop, rows, :] = speeds[index, start:stop]
            speed[start:stop] = speed[start:stop] * inside[start:stop]

    @pl.when(jnp.logical_not(has_left))
    def _():
        halo[:, :, 0] = jnp.zeros((STEPS, 2, REACH, rows_y, rows_z), jnp.float32)

    @pl.when(jnp.logical_not(has_right))
    def _():
        halo[:, :, 1] = jnp.zeros((STEPS, 2, REACH, rows_y, rows_z), jnp.float32)

    total[...] = jnp.zeros(total.shape, jnp.float32)
    global_x = space * cells_x + lax.broadcasted_iota(jnp.int32, inside.shape, 0)
    within = (global_x >= aperture[0, 0]) & (global_x < aperture[0, 1])
    inside[...] = jnp.where(within, 1.0, 0.0)

    def spread(now, field):
        cells = out[now, field].reshape(flat)
        high = cells.astype(jnp.bfloat16)
        low = (cells - high.astype(jnp.float32)).astype(jnp.bfloat16)
        lap[field] = (
            jnp.dot(left_ref[...], jnp.concatenate([high, low, high], axis=0), preferred_element_type=jnp.float32)
            + jnp.dot(jnp.concatenate([high, low, high], axis=1), right_ref[...], preferred_element_type=jnp.float32)
            + (3.0 * coefficients[0]) * cells
        ).reshape(lap.shape[1:])

    def advance(now, then, field, start, stop, beside=None):
        cells = slice(start, stop)
        summed = lap[field, cells]
        if beside is not None:
            summed = summed + beside
        following = (
            inside[cells] * (2.0 * out[now, field, cells] - out[then, field, cells])
            + speed[cells] * summed
        )
        out[then, field, cells] = following
        if field == 1:
            total[cells] = total[cells] + out[then, 0, cells] * following

    def border(index, now, then, field, side):
        received(out.at[now], index, field, side)
        for cell in range(REACH):
            if side == 0:
                at = cell
                beside = sum(
                    coefficients[cell + REACH - layer] * halo[index, field, 0, layer]
                    for layer in range(cell, REACH)
                )
            else:
                at = cells_x - REACH + cell
                beside = sum(
                    coefficients[REACH + layer - cell] * halo[index, field, 1, layer]
                    for layer in range(cell + 1)
                )
            advance(now, then, field, at, at + 1, beside[None])

    def step(index, carry):
        then = lax.rem(index, 2)
        now = 1 - then
        for field in range(2):
            @pl.when(index > 1)
            def _():
                sent(out.at[then], index - 1, field)

            @pl.when(index == 1)
            def _():
                sent(waves.at[1], 0, field)

            advance(now, then, field, REACH, cells_x - REACH)
            for side in range(2):
                border(index, now, then, field, side)
                send(out.at[then], index + 1, field, side)
            spread(then, field)
        return carry

    load.wait()
    load_left.wait()
    load_right.wait()
    spread(1, 0)
    spread(1, 1)
    own_speed.wait()
    gather((0, 1))
    for field in range(2):
        for side in range(2):
            border(0, 1, 0, field, side)
            send(out.at[0], 1, field, side)
    gather((2,))
    for field in range(2):
        advance(1, 0, field, REACH, cells_x - REACH)
        spread(0, field)

    lax.fori_loop(1, STEPS - 1, step, 0)

    last = STEPS - 1
    then = last % 2
    now = 1 - then
    keep_now = pltpu.make_async_copy(out.at[now], finals.at[0], local_sem.at[0])
    keep_now.start()

    def part_copy(kind, source, target, ahead):
        peer = lax.rem(shot + ahead, shots)
        return pltpu.make_async_remote_copy(
            source.at[peer],
            target.at[ahead - 1],
            part_send.at[kind, ahead - 1],
            part_recv.at[kind, ahead - 1],
            device_id={"shot": peer},
            device_id_type=pl.DeviceIdType.MESH,
        )

    for field in range(2):
        sent(out.at[then], last - 1, field)
        advance(now, then, field, REACH, cells_x - REACH)
    for index in range(shots):
        rows = slice(index * slab, (index + 1) * slab)
        middle[index] = total[REACH : cells_x - REACH, rows, :]
    copies = [part_copy(0, middle, middle_arrived, ahead) for ahead in range(1, shots)]
    for copy in copies:
        copy.start()
    for field in range(2):
        for side in range(2):
            border(last, now, then, field, side)
    for index in range(shots):
        rows = slice(index * slab, (index + 1) * slab)
        edges[index, 0:REACH] = total[0:REACH, rows, :]
        edges[index, REACH:] = total[cells_x - REACH :, rows, :]
    edge_copies = [part_copy(1, edges, edges_arrived, ahead) for ahead in range(1, shots)]
    for copy in edge_copies:
        copy.start()
    keep_then = pltpu.make_async_copy(out.at[then], finals.at[1], local_sem.at[1])
    keep_then.start()
    for field in range(2):
        sent(out.at[now], last, field)
    summed = middle[shot]
    for copy, ahead in zip(copies, range(1, shots)):
        copy.wait()
        summed = summed + middle_arrived[ahead - 1]
    image[REACH : cells_x - REACH] = summed / STEPS
    summed = edges[shot]
    for copy, ahead in zip(edge_copies, range(1, shots)):
        copy.wait()
        summed = summed + edges_arrived[ahead - 1]
    image[0:REACH] = summed[0:REACH] / STEPS
    image[cells_x - REACH :] = summed[REACH:] / STEPS
    keep_now.wait()
    keep_then.wait()


def keep(fields, image, fields_out, image_out, fields_held, image_held, load_sem, store_sem):
    pieces = [(image, image_held, image_out)]
    for time in range(2):
        for field in range(2):
            pieces.append(
                (fields.at[time, field], fields_held.at[time, field], fields_out.at[time, field])
            )
    loads = [
        pltpu.make_async_copy(source, held, load_sem.at[at])
        for at, (source, held, _) in enumerate(pieces)
    ]
    stores = [
        pltpu.make_async_copy(held, target, store_sem.at[at])
        for at, (_, held, target) in enumerate(pieces)
    ]
    for load in loads:
        load.start()
    for load, store in zip(loads, stores):
        load.wait()
        store.start()
    for store in stores:
        store.wait()


def shards(wavefields, velocity, aperture):
    fields = wavefields[0]
    cells_x, rows_y, rows_z = fields.shape[2:]
    shots = lax.axis_size("shot")
    slab = velocity.shape[1]
    left = split(
        np.kron(band(cells_x), np.eye(rows_y, dtype=np.float32))
        + np.kron(np.eye(cells_x, dtype=np.float32), band(rows_y)),
        1,
    )
    right = split(band(rows_z), 0)
    grid = (cells_x, rows_y, rows_z)
    vmem = pl.BlockSpec(memory_space=pltpu.VMEM)
    anywhere = pl.BlockSpec(memory_space=pl.ANY)
    finals, image = pl.pallas_call(
        kernel,
        out_shape=(
            jax.ShapeDtypeStruct(fields.shape, jnp.float32),
            jax.ShapeDtypeStruct(velocity.shape, jnp.float32),
        ),
        in_specs=[anywhere, anywhere, anywhere, anywhere, pl.BlockSpec(memory_space=pltpu.SMEM)],
        out_specs=(anywhere, vmem),
        scratch_shapes=[
            pltpu.VMEM(left.shape, jnp.bfloat16),
            pltpu.VMEM(right.shape, jnp.bfloat16),
            pltpu.VMEM(fields.shape, jnp.float32),
            pltpu.VMEM((STEPS, 2, 2, REACH, rows_y, rows_z), jnp.float32),
            pltpu.VMEM((shots,) + velocity.shape, jnp.float32),
            pltpu.VMEM(grid, jnp.float32),
            pltpu.VMEM(grid, jnp.float32),
            pltpu.VMEM((2,) + grid, jnp.float32),
            pltpu.VMEM(grid, jnp.float32),
            pltpu.VMEM((shots, cells_x - 2 * REACH, slab, rows_z), jnp.float32),
            pltpu.VMEM((shots - 1, cells_x - 2 * REACH, slab, rows_z), jnp.float32),
            pltpu.VMEM((shots, 2 * REACH, slab, rows_z), jnp.float32),
            pltpu.VMEM((shots - 1, 2 * REACH, slab, rows_z), jnp.float32),
            pltpu.SemaphoreType.DMA((STEPS, 2, 2)),
            pltpu.SemaphoreType.DMA((STEPS, 2, 2)),
            pltpu.SemaphoreType.DMA((3, shots - 1)),
            pltpu.SemaphoreType.DMA((3, shots - 1)),
            pltpu.SemaphoreType.DMA((2, shots - 1)),
            pltpu.SemaphoreType.DMA((2, shots - 1)),
            pltpu.SemaphoreType.DMA((4,)),
        ],
        compiler_params=pltpu.CompilerParams(collective_id=0, has_side_effects=True),
    )(jnp.asarray(left), jnp.asarray(right), fields, velocity, aperture)
    finals, image = pl.pallas_call(
        keep,
        out_shape=(
            jax.ShapeDtypeStruct(fields.shape, jnp.float32),
            jax.ShapeDtypeStruct(velocity.shape, jnp.float32),
        ),
        in_specs=[anywhere, anywhere],
        out_specs=(anywhere, anywhere),
        scratch_shapes=[
            pltpu.VMEM(fields.shape, jnp.float32),
            pltpu.VMEM(velocity.shape, jnp.float32),
            pltpu.SemaphoreType.DMA((5,)),
            pltpu.SemaphoreType.DMA((5,)),
        ],
    )(finals, image)
    return finals[None], image


def solution(mesh):
    in_specs = (
        P(("groups", "shot"), None, None, "space", None, None),
        P(("groups", "space"), "shot", None),
        P(("groups", "shot"), None),
    )
    out_specs = (
        P(("groups", "shot"), None, None, "space", None, None),
        P(("groups", "space"), "shot", None),
    )
    return jax.shard_map(shards, mesh=mesh, in_specs=in_specs, out_specs=out_specs, check_vma=False)
```

```python
import functools

import jax
import jax.numpy as jnp
import numpy as np
from jax import lax
from jax.experimental import pallas as pl
from jax.experimental.pallas import tpu as pltpu
from jax.sharding import PartitionSpec as P

STEPS = 8
REACH = 4


coefficients = (-205.0 / 72.0, 8.0 / 5.0, -1.0 / 5.0, 8.0 / 315.0, -1.0 / 560.0)


def band(size):
    matrix = np.zeros((size, size), np.float32)
    for reach in range(1, REACH + 1):
        matrix += np.float32(coefficients[reach]) * (
            np.eye(size, k=reach, dtype=np.float32) + np.eye(size, k=-reach, dtype=np.float32)
        )
    return matrix


def split(matrix, axis):
    high = matrix.astype(jnp.bfloat16)
    low = (matrix - high.astype(np.float32)).astype(jnp.bfloat16)
    return np.concatenate([high, high, low], axis=axis)


def kernel(
    left, right, waves, velocity, aperture, finals, image,
    left_ref, right_ref, out, halo, speeds, speed, inside, lap, total,
    middle, middle_arrived, edges, edges_arrived,
    halo_send, halo_recv, speed_send, speed_recv, part_send, part_recv, local_sem,
):
    space = lax.axis_index("space")
    spaces = lax.axis_size("space")
    shot = lax.axis_index("shot")
    shots = lax.axis_size("shot")
    cells_x, rows_y, rows_z = out.shape[2:]
    slab = velocity.shape[1]
    flat = (cells_x * rows_y, rows_z)
    has_left = space > 0
    has_right = space < spaces - 1

    load = pltpu.make_async_copy(waves, out, local_sem.at[0])
    load.start()
    load_left = pltpu.make_async_copy(left, left_ref, local_sem.at[2])
    load_left.start()
    load_right = pltpu.make_async_copy(right, right_ref, local_sem.at[3])
    load_right.start()
    own_speed = pltpu.make_async_copy(velocity, speeds.at[shot], local_sem.at[1])
    own_speed.start()

    barrier = pltpu.get_barrier_semaphore()

    @pl.when(has_left)
    def _():
        pl.semaphore_signal(barrier, inc=1, device_id={"space": space - 1}, device_id_type=pl.DeviceIdType.MESH)

    @pl.when(has_right)
    def _():
        pl.semaphore_signal(barrier, inc=1, device_id={"space": space + 1}, device_id_type=pl.DeviceIdType.MESH)

    for ahead in range(1, shots):
        peer = lax.rem(shot + ahead, shots)
        pl.semaphore_signal(barrier, inc=1, device_id={"shot": peer}, device_id_type=pl.DeviceIdType.MESH)
    pl.semaphore_wait(barrier, shots - 1 + jnp.where(has_left, 1, 0) + jnp.where(has_right, 1, 0))

    def to_right(source, slot, field):
        return pltpu.make_async_remote_copy(
            source.at[field, cells_x - REACH : cells_x],
            halo.at[slot, field, 0],
            halo_send.at[slot, field, 0],
            halo_recv.at[slot, field, 0],
            device_id={"space": space + 1},
            device_id_type=pl.DeviceIdType.MESH,
        )

    def to_left(source, slot, field):
        return pltpu.make_async_remote_copy(
            source.at[field, 0:REACH],
            halo.at[slot, field, 1],
            halo_send.at[slot, field, 1],
            halo_recv.at[slot, field, 1],
            device_id={"space": space - 1},
            device_id_type=pl.DeviceIdType.MESH,
        )

    def send(source, slot, field, side):
        if side == 0:
            @pl.when(has_left)
            def _():
                to_left(source, slot, field).start()
        else:
            @pl.when(has_right)
            def _():
                to_right(source, slot, field).start()

    def sent(source, slot, field):
        @pl.when(has_right)
        def _():
            to_right(source, slot, field).wait_send()

        @pl.when(has_left)
        def _():
            to_left(source, slot, field).wait_send()

    def received(source, slot, field, side):
        if side == 0:
            @pl.when(has_left)
            def _():
                to_right(source, slot, field).wait_recv()
        else:
            @pl.when(has_right)
            def _():
                to_left(source, slot, field).wait_recv()

    for field in range(2):
        for side in range(2):
            send(waves.at[1], 0, field, side)

    spans = ((0, REACH), (cells_x - REACH, cells_x), (REACH, cells_x - REACH))
    speed_copies = []
    for kind, (start, stop) in enumerate(spans):
        for ahead in range(1, shots):
            peer = lax.rem(shot + ahead, shots)
            copy = pltpu.make_async_remote_copy(
                velocity.at[start:stop],
                speeds.at[shot, start:stop],
                speed_send.at[kind, ahead - 1],
                speed_recv.at[kind, ahead - 1],
                device_id={"shot": peer},
                device_id_type=pl.DeviceIdType.MESH,
            )
            copy.start()
            speed_copies.append(copy)

    def gather(kinds):
        for kind in kinds:
            start, stop = spans[kind]
            for copy in speed_copies[kind * (shots - 1) : (kind + 1) * (shots - 1)]:
                copy.wait()
            for index in range(shots):
                rows = slice(index * slab, (index + 1) * slab)
                speed[start:stop, rows, :] = speeds[index, start:stop]
            speed[start:stop] = speed[start:stop] * inside[start:stop]

    @pl.when(jnp.logical_not(has_left))
    def _():
        halo[:, :, 0] = jnp.zeros((STEPS, 2, REACH, rows_y, rows_z), jnp.float32)

    @pl.when(jnp.logical_not(has_right))
    def _():
        halo[:, :, 1] = jnp.zeros((STEPS, 2, REACH, rows_y, rows_z), jnp.float32)

    total[...] = jnp.zeros(total.shape, jnp.float32)
    global_x = space * cells_x + lax.broadcasted_iota(jnp.int32, inside.shape, 0)
    within = (global_x >= aperture[0, 0]) & (global_x < aperture[0, 1])
    inside[...] = jnp.where(within, 1.0, 0.0)

    def spread(now, field):
        cells = out[now, field].reshape(flat)
        high = cells.astype(jnp.bfloat16)
        low = (cells - high.astype(jnp.float32)).astype(jnp.bfloat16)
        lap[field] = (
            jnp.dot(left_ref[...], jnp.concatenate([high, low, high], axis=0), preferred_element_type=jnp.float32)
            + jnp.dot(jnp.concatenate([high, low, high], axis=1), right_ref[...], preferred_element_type=jnp.float32)
            + (3.0 * coefficients[0]) * cells
        ).reshape(lap.shape[1:])

    def advance(now, then, field, start, stop, beside=None):
        cells = slice(start, stop)
        summed = lap[field, cells]
        if beside is not None:
            summed = summed + beside
        following = (
            inside[cells] * (2.0 * out[now, field, cells] - out[then, field, cells])
            + speed[cells] * summed
        )
        out[then, field, cells] = following
        if field == 1:
            total[cells] = total[cells] + out[then, 0, cells] * following

    def border(index, now, then, field, side):
        received(out.at[now], index, field, side)
        for cell in range(REACH):
            if side == 0:
                at = cell
                beside = sum(
                    coefficients[cell + REACH - layer] * halo[index, field, 0, layer]
                    for layer in range(cell, REACH)
                )
            else:
                at = cells_x - REACH + cell
                beside = sum(
                    coefficients[REACH + layer - cell] * halo[index, field, 1, layer]
                    for layer in range(cell + 1)
                )
            advance(now, then, field, at, at + 1, beside[None])

    def step(index, carry):
        then = lax.rem(index, 2)
        now = 1 - then
        for field in range(2):
            @pl.when(index > 1)
            def _():
                sent(out.at[then], index - 1, field)

            @pl.when(index == 1)
            def _():
                sent(waves.at[1], 0, field)

            for side in range(2):
                border(index, now, then, field, side)
                send(out.at[then], index + 1, field, side)
            advance(now, then, field, REACH, cells_x - REACH)
            spread(then, field)
        return carry

    load.wait()
    load_left.wait()
    load_right.wait()
    spread(1, 0)
    spread(1, 1)
    own_speed.wait()
    gather((0, 1))
    for field in range(2):
        for side in range(2):
            border(0, 1, 0, field, side)
            send(out.at[0], 1, field, side)
    gather((2,))
    for field in range(2):
        advance(1, 0, field, REACH, cells_x - REACH)
        spread(0, field)

    lax.fori_loop(1, STEPS - 1, step, 0)

    last = STEPS - 1
    then = last % 2
    now = 1 - then
    keep_now = pltpu.make_async_copy(out.at[now], finals.at[0], local_sem.at[0])
    keep_now.start()

    def part_copy(kind, source, target, ahead):
        peer = lax.rem(shot + ahead, shots)
        return pltpu.make_async_remote_copy(
            source.at[peer],
            target.at[ahead - 1],
            part_send.at[kind, ahead - 1],
            part_recv.at[kind, ahead - 1],
            device_id={"shot": peer},
            device_id_type=pl.DeviceIdType.MESH,
        )

    for field in range(2):
        sent(out.at[then], last - 1, field)
        advance(now, then, field, REACH, cells_x - REACH)
    for index in range(shots):
        rows = slice(index * slab, (index + 1) * slab)
        middle[index] = total[REACH : cells_x - REACH, rows, :]
    copies = [part_copy(0, middle, middle_arrived, ahead) for ahead in range(1, shots)]
    for copy in copies:
        copy.start()
    for field in range(2):
        for side in range(2):
            border(last, now, then, field, side)
    for index in range(shots):
        rows = slice(index * slab, (index + 1) * slab)
        edges[index, 0:REACH] = total[0:REACH, rows, :]
        edges[index, REACH:] = total[cells_x - REACH :, rows, :]
    edge_copies = [part_copy(1, edges, edges_arrived, ahead) for ahead in range(1, shots)]
    for copy in edge_copies:
        copy.start()
    keep_then = pltpu.make_async_copy(out.at[then], finals.at[1], local_sem.at[1])
    keep_then.start()
    for field in range(2):
        sent(out.at[now], last, field)
    summed = middle[shot]
    for copy, ahead in zip(copies, range(1, shots)):
        copy.wait()
        summed = summed + middle_arrived[ahead - 1]
    image[REACH : cells_x - REACH] = summed / STEPS
    summed = edges[shot]
    for copy, ahead in zip(edge_copies, range(1, shots)):
        copy.wait()
        summed = summed + edges_arrived[ahead - 1]
    image[0:REACH] = summed[0:REACH] / STEPS
    image[cells_x - REACH :] = summed[REACH:] / STEPS
    keep_now.wait()
    keep_then.wait()


def keep(fields, image, fields_out, image_out, fields_held, image_held, load_sem, store_sem):
    pieces = [(image, image_held, image_out)]
    for time in range(2):
        for field in range(2):
            pieces.append(
                (fields.at[time, field], fields_held.at[time, field], fields_out.at[time, field])
            )
    loads = [
        pltpu.make_async_copy(source, held, load_sem.at[at])
        for at, (source, held, _) in enumerate(pieces)
    ]
    stores = [
        pltpu.make_async_copy(held, target, store_sem.at[at])
        for at, (_, held, target) in enumerate(pieces)
    ]
    for load in loads:
        load.start()
    for load, store in zip(loads, stores):
        load.wait()
        store.start()
    for store in stores:
        store.wait()


def shards(wavefields, velocity, aperture):
    fields = wavefields[0]
    cells_x, rows_y, rows_z = fields.shape[2:]
    shots = lax.axis_size("shot")
    slab = velocity.shape[1]
    left = split(
        np.kron(band(cells_x), np.eye(rows_y, dtype=np.float32))
        + np.kron(np.eye(cells_x, dtype=np.float32), band(rows_y)),
        1,
    )
    right = split(band(rows_z), 0)
    grid = (cells_x, rows_y, rows_z)
    vmem = pl.BlockSpec(memory_space=pltpu.VMEM)
    anywhere = pl.BlockSpec(memory_space=pl.ANY)
    finals, image = pl.pallas_call(
        kernel,
        out_shape=(
            jax.ShapeDtypeStruct(fields.shape, jnp.float32),
            jax.ShapeDtypeStruct(velocity.shape, jnp.float32),
        ),
        in_specs=[anywhere, anywhere, anywhere, anywhere, pl.BlockSpec(memory_space=pltpu.SMEM)],
        out_specs=(anywhere, vmem),
        scratch_shapes=[
            pltpu.VMEM(left.shape, jnp.bfloat16),
            pltpu.VMEM(right.shape, jnp.bfloat16),
            pltpu.VMEM(fields.shape, jnp.float32),
            pltpu.VMEM((STEPS, 2, 2, REACH, rows_y, rows_z), jnp.float32),
            pltpu.VMEM((shots,) + velocity.shape, jnp.float32),
            pltpu.VMEM(grid, jnp.float32),
            pltpu.VMEM(grid, jnp.float32),
            pltpu.VMEM((2,) + grid, jnp.float32),
            pltpu.VMEM(grid, jnp.float32),
            pltpu.VMEM((shots, cells_x - 2 * REACH, slab, rows_z), jnp.float32),
            pltpu.VMEM((shots - 1, cells_x - 2 * REACH, slab, rows_z), jnp.float32),
            pltpu.VMEM((shots, 2 * REACH, slab, rows_z), jnp.float32),
            pltpu.VMEM((shots - 1, 2 * REACH, slab, rows_z), jnp.float32),
            pltpu.SemaphoreType.DMA((STEPS, 2, 2)),
            pltpu.SemaphoreType.DMA((STEPS, 2, 2)),
            pltpu.SemaphoreType.DMA((3, shots - 1)),
            pltpu.SemaphoreType.DMA((3, shots - 1)),
            pltpu.SemaphoreType.DMA((2, shots - 1)),
            pltpu.SemaphoreType.DMA((2, shots - 1)),
            pltpu.SemaphoreType.DMA((4,)),
        ],
        compiler_params=pltpu.CompilerParams(collective_id=0, has_side_effects=True),
    )(jnp.asarray(left), jnp.asarray(right), fields, velocity, aperture)
    finals, image = pl.pallas_call(
        keep,
        out_shape=(
            jax.ShapeDtypeStruct(fields.shape, jnp.float32),
            jax.ShapeDtypeStruct(velocity.shape, jnp.float32),
        ),
        in_specs=[anywhere, anywhere],
        out_specs=(anywhere, anywhere),
        scratch_shapes=[
            pltpu.VMEM(fields.shape, jnp.float32),
            pltpu.VMEM(velocity.shape, jnp.float32),
            pltpu.SemaphoreType.DMA((5,)),
            pltpu.SemaphoreType.DMA((5,)),
        ],
    )(finals, image)
    return finals[None], image


def solution(mesh):
    in_specs = (
        P(("groups", "shot"), None, None, "space", None, None),
        P(("groups", "space"), "shot", None),
        P(("groups", "shot"), None),
    )
    out_specs = (
        P(("groups", "shot"), None, None, "space", None, None),
        P(("groups", "space"), "shot", None),
    )
    return jax.shard_map(shards, mesh=mesh, in_specs=in_specs, out_specs=out_specs, check_vma=False)
```
